32 devices in a mesh: groups: 1, seq: 16 (over z, y, x), section: 1, head: 2 (over core).
Axes of the slice: x: 2, y: 2, z: 4, core: 2. Of those that a mesh axis runs over, the one named last changes fastest.
Arguments:
- queries: bfloat16 [2560, 3072], P(('groups', 'seq', 'head'), 'section'), may hold values from -24 to 24
- keys: bfloat16 [2560, 3072], P(('groups', 'seq', 'head'), 'section'), may hold values from -10.5 to 10.5
- values: bfloat16 [2560, 3072], P(('groups', 'seq', 'head'), 'section'), may hold values from -6 to 6
- text_keys: bfloat16 [128, 3072], P(('groups', 'seq', 'head'), 'section'), may hold values from -10 to 10
- text_values: bfloat16 [128, 3072], P(('groups', 'seq', 'head'), 'section'), may hold values from -6 to 6
- text_length: int32 [1], P('groups'), may hold values from 32 to 128
- out_weight: bfloat16 [3072, 3072], P(None, 'section'), may hold values from -0.109375 to 0.109375
Outputs:
- projected: bfloat16 [2560, 3072], P(('groups', 'seq', 'head'), 'section')
The draws below stay inside these ranges and needn't reach their ends.
All inputs are finite; a program needn't handle non-finite values.
Results may differ from the reference program's by a relative error of at most 0.0065.
Values may be sent and summed in bfloat16 or wider, within the bound.
No kernel may reach another device: no remote copies, remote signals or barrier semaphores. Data moves between devices by JAX's collectives and lax.ppermute only.
A program may use at most 128 MiB of HBM per device.

```python
import jax
import jax.numpy as jnp
from jax import lax

HEADS = 24
HEAD_DIM = 128
D = 3072
TXT = 128
TOKENS = 2560


spread = 1.7


def paired_draw(key):
    base = jax.random.fold_in(key, 41)
    query_key, keys_key = jax.random.split(base)
    query_draw = spread * jax.random.truncated_normal(query_key, -6.0, 6.0, (TOKENS, D), jnp.float32)
    keys_draw = spread * jax.random.truncated_normal(keys_key, -6.0, 6.0, (TOKENS, D), jnp.float32)
    return (query_draw, keys_draw)


def draw_queries(key, part):
    return paired_draw(key)[0].astype(jnp.bfloat16)


def draw_keys(key, part):
    return paired_draw(key)[1].astype(jnp.bfloat16)


def level_of(own_key, dims, pieces, least, high):
    def one(dim, blocks):
        steps = jax.random.uniform(jax.random.fold_in(jax.random.fold_in(own_key, 6), dim), (blocks,), jnp.float32, least / len(pieces), high / len(pieces))
        return jnp.repeat(jnp.exp(steps), dims[dim] // blocks).reshape((-1,) + (1,) * (len(dims) - dim - 1))

    factor_of = one(*pieces[0])
    for cut in pieces[1:]:
        factor_of = factor_of * one(*cut)
    return factor_of


def scatter_about(stream_key, dims, scale, limit, cuts=(), kind=jnp.bfloat16):
    array = jax.random.normal(stream_key, dims, jnp.float32) * scale
    if len(cuts) > 0:
        array = level_of(stream_key, dims, cuts, -0.22, 0.18) * array
    return jnp.clip(array, min=-limit, max=limit).astype(kind)


def setup_inputs(seed: int = 0, part: int = 0) -> dict:
    seeds = jax.random.split(jax.random.key(seed), 8)
    own_keys = jax.random.split(jax.random.fold_in(seeds[7], part), 8)
    queries = draw_queries(jax.random.fold_in(jax.random.fold_in(seeds[7], part), 71), part)
    keys = draw_keys(jax.random.fold_in(jax.random.fold_in(seeds[7], part), 71), part)
    values = scatter_about(own_keys[2], (TOKENS, D), 1.0, 6.0, ((0, 32),))
    text_keys = scatter_about(own_keys[3], (TXT, D), 1.7, 10.0, ((0, 32),))
    text_values = scatter_about(own_keys[4], (TXT, D), 1.0, 6.0, ((0, 32),))
    text_length = jax.random.randint(own_keys[5], (1,), TXT // 4, TXT + 1).astype(jnp.int32)
    out_weight = scatter_about(seeds[6], (D, D), D ** -0.5, 0.109375)
    return dict(queries=queries, keys=keys, values=values, text_keys=text_keys, text_values=text_values, text_length=text_length, out_weight=out_weight)


def reference(queries, keys, values, text_keys, text_values, text_length, out_weight):
    all_keys = jnp.concatenate([text_keys, keys], axis=0)
    all_values = jnp.concatenate([text_values, values], axis=0)
    usable = jnp.concatenate([jnp.arange(TXT) < text_length[0], jnp.ones((TOKENS,), dtype=bool)])
    queries_heads = queries.reshape(TOKENS, HEADS, HEAD_DIM).transpose(1, 0, 2)
    keys_heads = all_keys.reshape(TXT + TOKENS, HEADS, HEAD_DIM).transpose(1, 0, 2)
    values_heads = all_values.reshape(TXT + TOKENS, HEADS, HEAD_DIM).transpose(1, 0, 2)

    def one_head(operands):
        query_rows, key_rows, value_rows = operands
        scores = jnp.dot(query_rows, key_rows.T, preferred_element_type=jnp.float32) * (HEAD_DIM ** -0.5)
        scores = jnp.where(usable[None, :], scores, -1e30)
        highest = jnp.max(scores, axis=-1, keepdims=True)
        weights = jnp.exp(scores - highest)
        totals = jnp.sum(weights, axis=-1, keepdims=True)
        summed = jnp.dot(weights.astype(jnp.bfloat16), value_rows, preferred_element_type=jnp.float32)
        return summed / totals

    outputs = lax.map(one_head, (queries_heads, keys_heads, values_heads))
    attended = outputs.transpose(1, 0, 2).reshape(TOKENS, D).astype(jnp.bfloat16)
    return jnp.dot(attended, out_weight, preferred_element_type=jnp.float32).astype(jnp.bfloat16)
```

```python
import functools
import math

import jax
import jax.numpy as jnp
from jax import lax
from jax.experimental import pallas as pl
from jax.experimental.pallas import tpu as pltpu
from jax.sharding import PartitionSpec as P

HEAD_DIM = 128
AXES = ("seq", "head")


def swap(value, devices, mask):
    return lax.ppermute(value, AXES, [(i, i ^ mask) for i in range(devices)])


def attention_kernel(codes, video, text, text_pad, meta_ref, q_ref, *refs):
    parts = len(codes)
    part_refs, (o_ref, k_ref, v_ref) = refs[:parts], refs[parts:]
    groups, query_rows, _ = q_ref.shape
    dense = groups * video
    for p, ref in enumerate(part_refs):
        k_ref[p * dense : (p + 1) * dense] = ref[:, :video].reshape(dense, HEAD_DIM)
        v_ref[p * dense : (p + 1) * dense] = ref[:, video : 2 * video].reshape(dense, HEAD_DIM)
        small = groups * text_pad
        both = ref[:, 2 * video :].astype(jnp.float32).reshape(small, HEAD_DIM)
        at = parts * dense + p * small
        k_ref[at : at + small] = both.astype(jnp.bfloat16)
        v_ref[at : at + small] = pltpu.roll(both, small - text, 0).astype(jnp.bfloat16)
    me, length = meta_ref[0], meta_ref[1]
    small = groups * text_pad
    place = lax.broadcasted_iota(jnp.int32, (1, parts * small), 1)
    part = place // small
    inner = place % small
    row = inner % text_pad
    code = (inner // text_pad) * parts
    for p, value in enumerate(codes):
        code = code + jnp.where(part == p, value, 0)
    source = jnp.bitwise_xor(code, me)
    usable = jnp.logical_and(row < text, source * text + row < length)
    factor = HEAD_DIM ** -0.5 * math.log2(math.e)
    contract = (((1,), (1,)), ((), ()))
    step = 2 if groups % 2 == 0 else 1
    for t in range(0, groups, step):
        rows = step * query_rows
        q = q_ref[t : t + step].reshape(rows, HEAD_DIM)
        wide = parts * dense
        s = lax.dot_general(q, k_ref[:wide], contract, preferred_element_type=jnp.float32)
        st = lax.dot_general(q, k_ref[wide:], contract, preferred_element_type=jnp.float32)
        st = jnp.where(usable, st, -1e30)
        top = jnp.maximum(jnp.max(s, axis=1, keepdims=True), jnp.max(st, axis=1, keepdims=True))
        w = jnp.exp2((s - top) * factor)
        wt = jnp.exp2((st - top) * factor)
        total = jnp.sum(w, axis=1, keepdims=True) + jnp.sum(wt, axis=1, keepdims=True)
        out = jnp.dot(w.astype(jnp.bfloat16), v_ref[:wide], preferred_element_type=jnp.float32)
        out = out + jnp.dot(wt.astype(jnp.bfloat16), v_ref[wide:], preferred_element_type=jnp.float32)
        o_ref[t : t + step] = (out / total).astype(jnp.bfloat16).reshape(step, query_rows, HEAD_DIM)


def attention(meta, q, parts, codes, video, text, text_pad):
    groups, query_rows, columns = q.shape
    depth = parts[0].shape[1]
    keys = len(parts) * groups * (video + text_pad)
    whole = lambda h, meta: (0, 0, h)
    return pl.pallas_call(
        functools.partial(attention_kernel, codes, video, text, text_pad),
        out_shape=jax.ShapeDtypeStruct(q.shape, jnp.bfloat16),
        grid_spec=pltpu.PrefetchScalarGridSpec(
            num_scalar_prefetch=1,
            grid=(columns // HEAD_DIM,),
            in_specs=[pl.BlockSpec((groups, query_rows, HEAD_DIM), whole)]
            + [pl.BlockSpec((groups, depth, HEAD_DIM), whole)] * len(parts),
            out_specs=pl.BlockSpec((groups, query_rows, HEAD_DIM), whole),
            scratch_shapes=[
                pltpu.VMEM((keys, HEAD_DIM), jnp.bfloat16),
                pltpu.VMEM((keys, HEAD_DIM), jnp.bfloat16),
            ],
        ),
        name="attention",
    )(meta, q, *parts)


def shards(devices, queries, keys, values, text_keys, text_values, text_length, out_weight):
    rows, width = queries.shape
    text = text_keys.shape[0]
    text_pad = -(-2 * text // 8) * 8
    groups = math.gcd(width // HEAD_DIM, devices)
    columns = width // groups
    members = devices // groups
    me = lax.axis_index(AXES)
    mine = me // members

    filler = [jnp.zeros((text_pad - 2 * text, width), jnp.bfloat16)] if text_pad > 2 * text else []
    stack = jnp.concatenate([queries, keys, values, text_keys, text_values] + filler, axis=0)
    got = []
    for m in range(groups):
        piece = lax.dynamic_slice_in_dim(stack, jnp.bitwise_xor(mine, m) * columns, columns, 1)
        got.append(swap(piece, devices, m * members) if m else piece)
    q = jnp.stack([g[:rows] for g in got])
    held, codes = [jnp.stack([g[rows:] for g in got])], [0]
    bit = members // 2
    while bit:
        held = held + [swap(h, devices, bit) for h in held]
        codes = codes + [c ^ bit for c in codes]
        bit //= 2
    meta = jnp.stack([me.astype(jnp.int32), text_length[0]])
    attended = attention(meta, q, held, tuple(codes), rows, text, text_pad)
    pieces = []
    for m in range(groups):
        pieces.append(swap(attended[m], devices, m * members) if m else attended[m])
    blank = jnp.zeros((rows, width), jnp.bfloat16)
    for m, piece in enumerate(pieces):
        blank = lax.dynamic_update_slice_in_dim(blank, piece, jnp.bitwise_xor(mine, m) * columns, 1)
    result = jnp.dot(
        lax.all_gather(blank, "section", axis=1, tiled=True),
        out_weight,
        preferred_element_type=jnp.float32,
    )
    return result.astype(jnp.bfloat16)


def solution(mesh):
    devices = mesh.shape["seq"] * mesh.shape["head"]
    tokens = P(("groups", "seq", "head"), "section")
    return jax.shard_map(
        functools.partial(shards, devices),
        mesh=mesh,
        in_specs=(tokens, tokens, tokens, tokens, tokens, P("groups"), P(None, "section")),
        out_specs=tokens,
        check_vma=False,
    )
```
